256 devices in a mesh: chain: 64 (over z, y, core), col: 4 (over x).
Axes of the slice: x: 4, y: 4, z: 8, core: 2. Of those that a mesh axis runs over, the one named last changes fastest.
Arguments:
- diagonal_blocks: float32 [192, 256, 256], P('chain', 'col'), may hold values from -2 to 6, as said below
- couplings: float32 [192, 256, 256], P('chain', 'col'), may hold values from -2 to 2
- right_sides: float32 [64, 192, 256], P('col', 'chain'), may hold values from -0.04 to 0.04
Outputs:
- solution: float32 [64, 192, 256], P('col', 'chain')
The draws below stay inside these ranges and needn't reach their ends.
Inputs may be any that keep to these rules, and one draw needn't show every extreme that they name: `diagonal_blocks`: each block is symmetric, and the block-tridiagonal matrix that the diagonal blocks form with the couplings is positive definite with every eigenvalue 0.0003 or more.
All inputs are finite; a program needn't handle non-finite values.
Results may differ from the reference program's by a relative error of at most 0.0003.
Values sent between devices are 32-bit elements; how exact they have to be, the bound alone decides.
A program may use at most 64 MiB of HBM per device.

```python
import math
import jax
import jax.numpy as jnp
from jax import lax

NB = 256
NRHS = 64
N_SLABS = 192


def wire_blocks(key):
    base_key = jax.random.fold_in(key, 7)
    key_diag, key_rot, key_shift = jax.random.split(base_key, 3)
    stack_shape = (N_SLABS + 1, NB, NB)
    noise_diag = jax.random.normal(key_diag, stack_shape, jnp.float32)
    hop_ratio = 1.0
    rotation_seed = jax.random.normal(key_rot, stack_shape, jnp.float32)
    rotation, _ = jnp.linalg.qr(rotation_seed)
    identity = jnp.eye(NB, dtype=jnp.float32)
    spread = 0.25 / math.sqrt(NB)
    onsite = identity + spread * noise_diag
    hopping = -hop_ratio * jnp.einsum('kij,kjl->kil', onsite, rotation, precision=lax.Precision.HIGHEST)
    shifts = jnp.exp(jax.random.uniform(key_shift, (N_SLABS, 1, 1), jnp.float32, math.log(0.0003), math.log(0.001)))
    keeping = (jnp.arange(N_SLABS) < N_SLABS - 1).astype(jnp.float32)[:, None, None]
    onsite_here = onsite[:N_SLABS]
    onsite_next = onsite[1:]
    hop_next = hopping[1:]
    gram = jnp.einsum('kji,kjl->kil', onsite_here, onsite_here, precision=lax.Precision.HIGHEST)
    gram = gram + keeping * jnp.einsum('kji,kjl->kil', hop_next, hop_next, precision=lax.Precision.HIGHEST)
    gram = gram + shifts * identity
    diagonal = 0.5 * (gram + jnp.swapaxes(gram, 1, 2))
    coupling = jnp.einsum('kji,kjl->kil', hop_next, onsite_next, precision=lax.Precision.HIGHEST)
    return (diagonal, coupling)


def draw_diagonal_blocks(key, part):
    return wire_blocks(key)[0]


def draw_couplings(key, part):
    return wire_blocks(key)[1]


def draw_right_sides(key, part):
    rough = jax.random.normal(jax.random.fold_in(key, 11), (NRHS, N_SLABS, NB), jnp.float32)
    return jnp.clip(0.005 * rough, -0.04, 0.04)


def setup_inputs(seed: int = 0) -> dict:
    arg_keys = jax.random.split(jax.random.key(seed), 4)
    diagonal_blocks = draw_diagonal_blocks(jax.random.fold_in(arg_keys[3], 71), 0)
    couplings = draw_couplings(jax.random.fold_in(arg_keys[3], 71), 0)
    right_sides = draw_right_sides(jax.random.fold_in(arg_keys[3], 71), 0)
    return {"diagonal_blocks": diagonal_blocks, "couplings": couplings, "right_sides": right_sides}


finest = lax.Precision.HIGHEST

def reference(diagonal_blocks, couplings, right_sides):
    loads = jnp.transpose(right_sides, (1, 2, 0))

    def forward(state, entries):
        factor_prev, solved_prev, coup_prev = state
        matrix, coup_now, load_now = entries
        schur_block = matrix - jnp.dot(coup_prev.T, factor_prev, precision=finest)
        reduced = load_now - jnp.dot(coup_prev.T, solved_prev, precision=finest)
        joined = jnp.linalg.solve(schur_block, jnp.concatenate([coup_now, reduced], axis=1))
        factor_now = joined[:, :NB]
        solved_now = joined[:, NB:]
        return ((factor_now, solved_now, coup_now), (factor_now, solved_now))
    start_state = (jnp.zeros((NB, NB), jnp.float32), jnp.zeros((NB, NRHS), jnp.float32), jnp.zeros((NB, NB), jnp.float32))
    _, (factors, solved) = lax.scan(forward, start_state, (diagonal_blocks, couplings, loads))

    def backward(after, entries):
        factor_now, solved_now = entries
        current = solved_now - jnp.dot(factor_now, after, precision=finest)
        return (current, current)
    last_rows = solved[-1]
    _, earlier = lax.scan(backward, last_rows, (factors[:-1], solved[:-1]), reverse=True)
    result = jnp.concatenate([earlier, last_rows[None]], axis=0)
    return jnp.transpose(result, (2, 0, 1))
```

```python
import functools

import jax
import jax.numpy as jnp
from jax import lax
from jax.experimental import pallas as pl
from jax.experimental.pallas import tpu as pltpu
from jax.sharding import PartitionSpec as P

MESH = pl.DeviceIdType.MESH
PIVOTS = 32
SUB = 8


def dot_nn(a, b):
    return lax.dot_general(
        a, b, (((1,), (0,)), ((), ())),
        precision=lax.Precision.HIGHEST, preferred_element_type=jnp.float32,
    )


def dot_nt(a, b):
    return lax.dot_general(
        a, b, (((1,), (1,)), ((), ())),
        precision=lax.Precision.HIGHEST, preferred_element_type=jnp.float32,
    )


def sweep_panel(block, panel):
    count = len(block)
    ids = lax.broadcasted_iota(jnp.int32, block[0].shape, 0)
    ids_wide = lax.broadcasted_iota(jnp.int32, panel[0].shape, 0)
    reps = panel[0].shape[1] // block[0].shape[1]

    def wide(v):
        return jnp.concatenate([v] * reps, axis=1)

    for at in range(count):
        cols = [
            [jnp.broadcast_to(g[:, at * SUB + j : at * SUB + j + 1], block[0].shape) for g in block]
            for j in range(SUB)
        ]
        for s in range(SUB):
            pivot_col = cols[s]
            inv_pivot = 1.0 / jnp.broadcast_to(pivot_col[at][s : s + 1, :], block[0].shape)
            factors = [c * inv_pivot for c in pivot_col]
            factors_wide = [wide(f) for f in factors]
            inv_wide = wide(inv_pivot)

            def eliminated(groups, facs, inv, hit):
                row = jnp.broadcast_to(groups[at][s : s + 1, :], groups[0].shape)
                out = [g - f * row for g, f in zip(groups, facs)]
                out[at] = jnp.where(hit, inv * row, out[at])
                return out

            for j in range(s + 1, SUB):
                cols[j] = eliminated(cols[j], factors, inv_pivot, ids == s)
            if at < count - 1:
                block = eliminated(block, factors, inv_pivot, ids == s)
            panel = eliminated(panel, factors_wide, inv_wide, ids_wide == s)
    return panel


def invert_in_place(ref, hook=None):
    size = ref.shape[0]
    lane = lax.broadcasted_iota(jnp.int32, (PIVOTS, size), 1)
    row = lax.broadcasted_iota(jnp.int32, (PIVOTS, size), 0)
    lane_low = lax.broadcasted_iota(jnp.int32, (size - PIVOTS, size), 1)
    unit = (lane == row).astype(jnp.float32)

    def step(i, carry):
        top = ref[0:PIVOTS, :]
        low = ref[PIVOTS:, :]
        start = jnp.where(lane < PIVOTS, unit, top)
        groups = range(0, PIVOTS, SUB)
        swept = sweep_panel(
            [top[g : g + SUB, 0:128] for g in groups], [start[g : g + SUB, :] for g in groups]
        )
        swept = jnp.concatenate(swept, axis=0)
        rest = jnp.where(lane_low < PIVOTS, 0.0, low) - dot_nn(low[:, 0:PIVOTS], swept)
        ref[0 : size - PIVOTS, :] = pltpu.roll(rest, size - PIVOTS, 1)
        ref[size - PIVOTS :, :] = pltpu.roll(swept, size - PIVOTS, 1)
        if hook is not None:
            @pl.when(i == 2)
            def _():
                hook()
        return carry

    lax.fori_loop(0, size // PIVOTS, step, 0)


def kernel(
    n, m, levels,
    diag, coup, loads, out,
    gath, inv0, inv1, work, c0t, f1, g1, wide0, wide1, hq, bq, dnb, dnh,
    send_b, send_fg, send_h, got_b, got_h, xb, xfg, sol, got_sol,
    s_first_send, s_first_recv, s_c2, s_sol,
    s_send, s_x_send, r_b, r_fg, r_h, r_xb, r_xfg,
):
    k = lax.axis_index("chain")
    x = lax.axis_index("col")
    q = diag.shape[1]
    size = diag.shape[2]
    nrhs = loads.shape[1]
    own = pl.ds(pl.multiple_of(x * q, q), q)
    has_up = k + 1 < n
    has_low = k >= 1

    def place(p):
        return pl.ds(pl.multiple_of(lax.rem(x + m - p, m) * q, q), q)

    def copy(src, dst, send, recv, chain, col):
        return pltpu.make_async_remote_copy(
            src_ref=src, dst_ref=dst, send_sem=send, recv_sem=recv,
            device_id=(chain, col), device_id_type=MESH,
        )

    def zero(ref):
        ref[...] = jnp.zeros(ref.shape, jnp.float32)

    @pl.when(jnp.logical_not(has_low))
    def _():
        zero(gath.at[4, own])

    def fill(e, d):
        @pl.when(k - d < 0)
        def _():
            zero(got_b.at[e, 0])
            zero(got_h.at[e, 0])
            zero(xfg.at[e, 0, own])

        @pl.when(k + d >= n)
        def _():
            zero(got_b.at[e, 1])
            zero(got_h.at[e, 1])
            zero(xfg.at[e, 1, own])

        return d * 2

    lax.fori_loop(1, levels + 1, fill, 1)

    @pl.when(jnp.logical_not(has_up))
    def _():
        zero(got_b.at[0, 1])
        zero(got_h.at[0, 1])
        zero(xfg.at[0, 1, own])

    barrier = pltpu.get_barrier_semaphore()
    partners = m - 1
    for p in range(1, m):
        pl.semaphore_signal(barrier, inc=1, device_id=(k, lax.rem(x + p, m)), device_id_type=MESH)
    for level in range(levels):
        d = 1 << level
        for cond, other in ((k + d < n, k + d), (k - d >= 0, k - d)):
            @pl.when(cond)
            def _():
                pl.semaphore_signal(barrier, inc=1, device_id=(other, x), device_id_type=MESH)
            partners = partners + cond.astype(jnp.int32)
    pl.semaphore_wait(barrier, partners)

    def first(i, src, p):
        return copy(src, gath.at[i, own], s_first_send.at[i, p - 1], s_first_recv.at[i, p - 1], k, lax.rem(x + p, m))

    def first_wait(i):
        for p in range(1, m):
            copy(
                gath.at[i, place(p)], gath.at[i, place(p)], s_first_send.at[i, p - 1], s_first_recv.at[i, p - 1],
                k, lax.rem(x + p, m),
            ).wait_recv()

    sources = (diag.at[0], coup.at[0], diag.at[1], coup.at[1], gath.at[4, own])
    for p in range(1, m):
        first(0, sources[0], p).start()

    def c2_copy():
        return copy(coup.at[2], gath.at[4, own], s_c2.at[0], s_c2.at[1], lax.rem(k + 1, n), x)

    @pl.when(has_up)
    def _():
        c2_copy().start()

    for i in range(1, 4):
        for p in range(1, m):
            first(i, sources[i], p).start()
    for i in range(4):
        gath[i, own] = sources[i][...]
    first_wait(0)

    inv0[...] = gath[0]

    def forward_c2():
        @pl.when(has_low)
        def _():
            c2_copy().wait_recv()

        for p in range(1, m):
            first(4, sources[4], p).start()

    invert_in_place(inv0, forward_c2)
    first_wait(1)
    first_wait(2)
    first_wait(4)
    c0 = gath[1]
    f0 = gath[4]
    inverse = inv0[...]
    c0t[...] = c0.T
    wide0[...] = dot_nn(f0, inverse)
    wide1[...] = dot_nn(c0t[...], inverse)
    f1[...] = -dot_nn(wide0[...], c0)
    inv1[...] = gath[2] - dot_nn(wide1[...], c0)
    wh0 = dot_nn(loads[0], inverse)
    hq[1] = loads[1] - dot_nn(wh0, c0)
    dnb[...] = dot_nt(wide0[own], f0)
    dnh[...] = dot_nt(wh0, f0)

    invert_in_place(inv1)
    first_wait(3)
    g1[...] = gath[3].T

    def chain_send(e, kind, side, d):
        other = lax.rem(k + d, n) if side == 0 else lax.rem(k - d + n, n)
        src, dst, recv = (
            (send_b.at[side], got_b.at[e, side], r_b),
            (send_fg.at[side], xfg.at[e, side, own], r_fg),
            (send_h.at[side], got_h.at[e, side], r_h),
        )[kind]
        return copy(src, dst, s_send.at[kind, side], recv.at[e, side], other, x)

    def spread(e, p):
        return copy(
            xb.at[e, own], xb.at[e, own], s_x_send.at[0, p - 1], r_xb.at[e, p - 1], k, lax.rem(x + p, m)
        )

    def spread_fg(e, p):
        return copy(
            xfg.at[e, :, own], xfg.at[e, :, own], s_x_send.at[1, p - 1], r_xfg.at[e, p - 1], k, lax.rem(x + p, m)
        )

    def spread_wait(e, p):
        copy(
            xb.at[e, place(p)], xb.at[e, place(p)], s_x_send.at[0, p - 1], r_xb.at[e, p - 1], k, lax.rem(x + p, m)
        ).wait_recv()

    def spread_fg_wait(e, p):
        copy(
            xfg.at[e, :, place(p)], xfg.at[e, :, place(p)], s_x_send.at[1, p - 1], r_xfg.at[e, p - 1],
            k, lax.rem(x + p, m),
        ).wait_recv()

    stacked = jnp.concatenate([f1[own], g1[own], hq[1]], axis=0)
    w = dot_nn(stacked, inv1[...])
    w_f, w_g, w_h = w[0:q], w[q : 2 * q], w[2 * q :]
    send_b[1] = dnb[...] + dot_nt(w_f, f1[...])
    @pl.when(has_low)
    def _():
        chain_send(0, 0, 1, 1).start()

    send_fg[1] = -dot_nt(w_g, f1[...])
    send_h[1] = dnh[...] + dot_nt(w_h, f1[...])
    @pl.when(has_low)
    def _():
        chain_send(0, 1, 1, 1).start()
        chain_send(0, 2, 1, 1).start()

    own_terms = dot_nt(w, g1[...])
    xfg[0, 0, own] = -own_terms[0:q]
    hq[2] = loads[2] - own_terms[2 * q :]
    local_b = diag[2] - own_terms[q : 2 * q]

    @pl.when(has_up)
    def _():
        chain_send(0, 0, 1, 1).wait_recv()

    bq[...] = local_b - got_b[0, 1]
    xb[0, own] = bq[...]
    for p in range(1, m):
        spread(0, p).start()

    @pl.when(has_low)
    def _():
        for kind in range(3):
            chain_send(0, kind, 1, 1).wait_send()

    zero(got_h.at[0, 0])

    def level(l, half):
        below = jnp.logical_and(l >= 1, k - half >= 0)
        above = k + half < n
        full = jnp.where(l == 0, 1, 2 * half)
        up_ok = k + full < n
        low_ok = k - full >= 0
        more = l < levels

        for p in range(1, m):
            spread_wait(l, p)
        work[...] = xb[l]

        def forward_fg():
            @pl.when(jnp.logical_and(above, more))
            def _():
                chain_send(l, 1, 1, half).wait_recv()

            @pl.when(jnp.logical_and(below, more))
            def _():
                chain_send(l, 1, 0, half).wait_recv()

            @pl.when(more)
            def _():
                for p in range(1, m):
                    spread_fg(l, p).start()

        invert_in_place(work, forward_fg)
        for p in range(1, m):
            spread(l, p).wait_send()

        @pl.when(above)
        def _():
            chain_send(l, 2, 1, half).wait_recv()

        @pl.when(below)
        def _():
            chain_send(l, 2, 0, half).wait_recv()

        hq[2] = hq[2] - got_h[l, 0] - got_h[l, 1]

        @pl.when(more)
        def _():
            for p in range(1, m):
                spread_fg_wait(l, p)
            stacked = jnp.concatenate([xfg[l, 0, own], xfg[l, 1, own], hq[2]], axis=0)
            w = dot_nn(stacked, work[...])
            send_b[1] = dot_nt(w[0:q], xfg[l, 0])
            send_b[0] = dot_nt(w[q : 2 * q], xfg[l, 1])

            @pl.when(low_ok)
            def _():
                chain_send(l + 1, 0, 1, full).start()

            @pl.when(up_ok)
            def _():
                chain_send(l + 1, 0, 0, full).start()

            to_low = dot_nt(w[q:], xfg[l, 0])
            send_fg[1] = -to_low[0:q]
            send_h[1] = to_low[q:]

            @pl.when(low_ok)
            def _():
                chain_send(l + 1, 2, 1, full).start()

            to_up_f = dot_nt(w[0:q], xfg[l, 1])
            send_fg[0] = -to_up_f
            send_h[0] = dot_nt(w[2 * q :], xfg[l, 1])

            @pl.when(up_ok)
            def _():
                chain_send(l + 1, 2, 0, full).start()

            @pl.when(jnp.logical_and(low_ok, l + 1 < levels))
            def _():
                chain_send(l + 1, 1, 1, full).start()

            @pl.when(jnp.logical_and(up_ok, l + 1 < levels))
            def _():
                chain_send(l + 1, 1, 0, full).start()

            @pl.when(up_ok)
            def _():
                chain_send(l + 1, 0, 1, full).wait_recv()

            @pl.when(low_ok)
            def _():
                chain_send(l + 1, 0, 0, full).wait_recv()

            bq[...] = bq[...] - got_b[l + 1, 0] - got_b[l + 1, 1]
            xb[l + 1, own] = bq[...]
            for p in range(1, m):
                spread(l + 1, p).start()

            @pl.when(low_ok)
            def _():
                chain_send(l + 1, 0, 1, full).wait_send()
                chain_send(l + 1, 2, 1, full).wait_send()

            @pl.when(up_ok)
            def _():
                chain_send(l + 1, 0, 0, full).wait_send()
                chain_send(l + 1, 2, 0, full).wait_send()

            @pl.when(jnp.logical_and(low_ok, l + 1 < levels))
            def _():
                chain_send(l + 1, 1, 1, full).wait_send()

            @pl.when(jnp.logical_and(up_ok, l + 1 < levels))
            def _():
                chain_send(l + 1, 1, 0, full).wait_send()

            for p in range(1, m):
                spread_fg(l, p).wait_send()

        return full

    lax.fori_loop(0, levels + 1, level, 1)

    sol[...] = dot_nn(hq[2], work[...])

    def sol_copy():
        return copy(sol, got_sol, s_sol.at[0], s_sol.at[1], lax.rem(k + 1, n), x)

    @pl.when(has_up)
    def _():
        sol_copy().start()

    @pl.when(jnp.logical_not(has_low))
    def _():
        zero(got_sol)

    out[2] = sol[...]
    part1 = hq[1] - dot_nn(sol[...], g1[...])

    @pl.when(has_low)
    def _():
        sol_copy().wait_recv()

    x1 = dot_nn(part1 - dot_nn(got_sol[...], f1[...]), inv1[...])
    out[1] = x1
    part0 = loads[0] - dot_nn(got_sol[...], gath[4])
    out[0] = dot_nn(part0 - dot_nn(x1, c0t[...]), inv0[...])

    @pl.when(has_up)
    def _():
        sol_copy().wait_send()
        c2_copy().wait_send()

    for i in range(5):
        for p in range(1, m):
            first(i, sources[i], p).wait_send()


def per_device(n, m, diagonal_blocks, couplings, right_sides):
    levels = n.bit_length() - 1
    slabs, q, size = diagonal_blocks.shape
    nrhs = right_sides.shape[0]
    loads = jnp.swapaxes(right_sides, 0, 1)
    steps = levels + 1

    def vmem(*shape):
        return pltpu.VMEM(shape, jnp.float32)

    def dma(*shape):
        return pltpu.SemaphoreType.DMA(shape)

    space = pl.BlockSpec(memory_space=pltpu.VMEM)
    result = pl.pallas_call(
        functools.partial(kernel, n, m, levels),
        out_shape=jax.ShapeDtypeStruct(loads.shape, jnp.float32),
        in_specs=[space] * 3,
        out_specs=space,
        scratch_shapes=[
            vmem(5, size, size), vmem(size, size), vmem(size, size), vmem(size, size),
            vmem(size, size), vmem(size, size), vmem(size, size), vmem(size, size), vmem(size, size),
            vmem(slabs, nrhs, size), vmem(q, size), vmem(q, size), vmem(nrhs, size),
            vmem(2, q, size), vmem(2, q, size), vmem(2, nrhs, size),
            vmem(steps, 2, q, size), vmem(steps, 2, nrhs, size),
            vmem(steps, size, size), vmem(steps, 2, size, size),
            vmem(nrhs, size), vmem(nrhs, size),
            dma(5, m - 1), dma(5, m - 1), dma(2), dma(2),
            dma(3, 2), dma(2, m - 1),
            dma(steps, 2), dma(steps, 2), dma(steps, 2), dma(steps, m - 1), dma(steps, m - 1),
        ],
        compiler_params=pltpu.CompilerParams(
            collective_id=0, has_side_effects=True, vmem_limit_bytes=40 * 1024 * 1024
        ),
    )(diagonal_blocks, couplings, loads)
    return jnp.swapaxes(result, 0, 1)


def solution(mesh):
    n, m = mesh.shape["chain"], mesh.shape["col"]
    return jax.shard_map(
        functools.partial(per_device, n, m),
        mesh=mesh,
        in_specs=(P("chain", "col", None), P("chain", "col", None), P("col", "chain", None)),
        out_specs=P("col", "chain", None),
        check_vma=False,
    )
```
